32 devices in a mesh: freq: 2 (over x), sec: 16 (over z, y, core).
Axes of the slice: x: 2, y: 2, z: 4, core: 2. Of those that a mesh axis runs over, the one named last changes fastest.
Arguments:
- layer_trans: bfloat16 [16, 1024, 1024], P('sec'), may hold values from -0.1875 to 0.1875
- layer_refl: bfloat16 [16, 1024, 1024], P('sec'), may hold values from -0.046875 to 0.046875
- source_modes: int32 [256], P('freq'), parts along dimension 0, may hold values from 0 to 1023
Outputs:
- upgoing: bfloat16 [32, 64, 1024], P(('freq', 'sec')), parts along dimension 0
The draws below stay inside these ranges and needn't reach their ends.
There are 2 independent parts, one for each index of `freq`. The reference program is written for one: setup_inputs(seed, part) draws one part's arguments, and reference() takes and returns one part's arrays. A program takes and returns all parts, laid end to end along the dimension named above; an argument that names none is the same for every part. Nothing has to cross between parts.
All inputs are finite; a program needn't handle non-finite values.
Results may differ from the reference program's by a relative error of at most 0.035.
Values may be sent and summed in bfloat16 or wider, within the bound.
No kernel may reach another device: no remote copies, remote signals or barrier semaphores. Data moves between devices by JAX's collectives and lax.ppermute only.
A program may use at most 64 MiB of HBM per device.

```python
import jax
import jax.numpy as jnp
from jax import lax

M = 1024
NSRC = 128
LAYERS = 16
N_SEC = 16


def touch_ends(entries, key, least, high):
    longest = entries.shape.index(max(entries.shape))
    spots = []
    for shift in (0, 1):
        where = [jax.random.randint(jax.random.fold_in(key, axis), (), 0, length) for axis, length in enumerate(entries.shape)]
        where[longest] = (where[longest] + shift) % entries.shape[longest]
        spots.append(tuple(where))
    return entries.at[spots[0]].set(least).at[spots[1]].set(high)


def levels(key, dims, pieces, low, largest):
    gain, own = 1.0, jax.random.fold_in(key, 6)
    for axis_at, shards_of in pieces:
        heights = jnp.exp(jax.random.uniform(jax.random.fold_in(own, axis_at), (shards_of,), jnp.float32, low / len(pieces), largest / len(pieces)))
        gain = gain * jnp.repeat(heights, dims[axis_at] // shards_of).reshape([-1 if axis == axis_at else 1 for axis in range(len(dims))])
    return gain


def gaussian(rng, shape, width, bound, shards=(), kind=jnp.bfloat16):
    drawn = jax.random.normal(rng, shape, jnp.float32) * width
    if len(shards) > 0:
        drawn = levels(rng, shape, shards, -0.22, 0.18) * drawn
    return jnp.clip(drawn, min=-bound, max=bound).astype(kind)


def setup_inputs(seed: int = 0, part: int = 0) -> dict:
    arg_keys = jax.random.split(jax.random.key(seed), 4)
    part_splits = jax.random.split(jax.random.fold_in(arg_keys[3], part), 4)
    return {
        "layer_trans": gaussian(arg_keys[0], (LAYERS, M, M), M ** -0.5, 0.1875, ((0, 16),)),
        "layer_refl": gaussian(arg_keys[1], (LAYERS, M, M), (M * LAYERS) ** -0.5, 0.046875, ((0, 16),)),
        "source_modes": touch_ends(jax.random.randint(part_splits[2], (NSRC,), 0, M), jax.random.fold_in(part_splits[2], 1), 0, M - 1).astype(jnp.int32),
    }


def reference(layer_trans, layer_refl, source_modes):
    def merge_pair(index):
        upper_t = lax.dynamic_index_in_dim(layer_trans, 2 * index, 0, keepdims=False).astype(jnp.float32)
        lower_t = lax.dynamic_index_in_dim(layer_trans, 2 * index + 1, 0, keepdims=False).astype(jnp.float32)
        upper_r = lax.dynamic_index_in_dim(layer_refl, 2 * index, 0, keepdims=False).astype(jnp.float32)
        lower_r = lax.dynamic_index_in_dim(layer_refl, 2 * index + 1, 0, keepdims=False).astype(jnp.float32)
        sect_t = jnp.dot(upper_t, lower_t, preferred_element_type=jnp.float32).astype(jnp.bfloat16)
        inner = jnp.dot(lower_r, upper_t.T, preferred_element_type=jnp.float32).astype(jnp.bfloat16)
        sect_r = (upper_r + jnp.dot(upper_t, inner.astype(jnp.float32), preferred_element_type=jnp.float32)).astype(jnp.bfloat16)
        return sect_t, sect_r

    sect_trans, sect_refl = lax.map(merge_pair, jnp.arange(N_SEC // 2, dtype=jnp.int32))
    down_first = (source_modes[:, None] == jnp.arange(M, dtype=jnp.int32)[None, :]).astype(jnp.bfloat16)

    def go_down(down, mats):
        sect_t, sect_r = mats
        down32 = down.astype(jnp.float32)
        echo = jnp.dot(down32, sect_r.astype(jnp.float32), preferred_element_type=jnp.float32)
        after = jnp.dot(down32, sect_t.astype(jnp.float32), preferred_element_type=jnp.float32).astype(jnp.bfloat16)
        return after, echo

    unused, echoes = lax.scan(go_down, down_first, (sect_trans, sect_refl))

    def go_up(upper, items):
        sect_t, echo = items
        value = (echo + jnp.dot(upper.astype(jnp.float32), sect_t.astype(jnp.float32).T, preferred_element_type=jnp.float32)).astype(jnp.bfloat16)
        return value, value

    start_up = jnp.zeros((NSRC, M), jnp.bfloat16)
    unused_up, ups = lax.scan(go_up, start_up, (sect_trans, echoes), reverse=True)
    return ups.reshape(N_SEC, NSRC // 2, M)
```

```python
import jax
import jax.numpy as jnp
from jax import lax
from jax.sharding import PartitionSpec as P


def swap_cores(array):
    return lax.ppermute(array, "sec", [(i, i ^ 1) for i in range(lax.axis_size("sec"))])


def swap_sections(value, one, two):
    pairs = []
    for device in range(lax.axis_size("sec")):
        section, core = divmod(device, 2)
        if section == one:
            target = 2 * two + core
        elif section == two:
            target = 2 * one + core
        else:
            target = device ^ 1
        pairs.append((device, target))
    return lax.ppermute(value, "sec", pairs)


def matmul(left, right):
    return jnp.dot(left, right, preferred_element_type=jnp.float32)


def matmul_nt(left, right):
    return lax.dot_general(
        left, right, (((1,), (1,)), ((), ())), preferred_element_type=jnp.float32
    )


def rounded(value):
    return value.astype(jnp.bfloat16)


def merge_trans(upper_t, lower_t):
    return rounded(matmul(upper_t, lower_t))


def echo_of(down, upper_t, upper_r, lower_r):
    through = rounded(matmul(down, upper_t))
    back = rounded(matmul(through, lower_r))
    return matmul(down, upper_r) + matmul_nt(back, upper_t)


def shards(layer_trans, layer_refl, source_modes):
    position = lax.axis_index("sec")
    section = position // 2
    parity = position % 2
    is_upper = parity == 0
    sections = lax.axis_size("sec") // 2
    trans = layer_trans[0]
    refl = layer_refl[0]
    half = source_modes.shape[0] // 2

    columns = jnp.arange(trans.shape[0], dtype=jnp.int32)
    units = rounded(source_modes[:, None] == columns[None, :])
    picked = rounded(matmul(units, trans))
    picked = swap_cores(picked)
    first = rounded(matmul(picked, trans))
    first = jnp.where(is_upper, swap_cores(first[:half]), first[half:])

    other_t = swap_cores(trans)
    other_r = swap_cores(refl)
    incoming = swap_sections(first, 0, 1)
    merged_t = lax.cond(
        is_upper,
        lambda: merge_trans(trans, other_t),
        lambda: merge_trans(other_t, trans),
    )
    mine = jnp.where(is_upper, units[:half], units[half:])
    mine = jnp.where(section == 1, incoming, mine)
    for step in range(1, sections - 1):
        incoming = swap_sections(rounded(matmul(incoming, merged_t)), step, step + 1)
        mine = jnp.where(section == step + 1, incoming, mine)

    echo = lax.cond(
        is_upper,
        lambda: echo_of(mine, trans, refl, other_r),
        lambda: echo_of(mine, other_t, other_r, refl),
    )

    value = rounded(echo)
    upgoing = value
    for step in range(sections - 2, -1, -1):
        incoming = swap_sections(value, step + 1, step)
        value = rounded(echo + matmul_nt(incoming, merged_t))
        upgoing = jnp.where(section == step, value, upgoing)
    return upgoing[None]


def solution(mesh):
    return jax.shard_map(
        shards,
        mesh=mesh,
        in_specs=(P("sec", None, None), P("sec", None, None), P("freq")),
        out_specs=P(("freq", "sec"), None, None),
        check_vma=False,
    )
```

```python
import jax
import jax.numpy as jnp
from jax import lax
from jax.experimental import pallas as pl
from jax.experimental.pallas import tpu as pltpu
from jax.sharding import PartitionSpec as P

BLOCKS = 4


def swap_cores(array):
    return lax.ppermute(array, "sec", [(i, i ^ 1) for i in range(lax.axis_size("sec"))])


def swap_sections(value, one, two):
    pairs = []
    for device in range(lax.axis_size("sec")):
        section, core = divmod(device, 2)
        if section == one:
            target = 2 * two + core
        elif section == two:
            target = 2 * one + core
        else:
            target = device ^ 1
        pairs.append((device, target))
    return lax.ppermute(value, "sec", pairs)


def matmul(left, right):
    return jnp.dot(left, right, preferred_element_type=jnp.float32)


def matmul_nt(left, right):
    return lax.dot_general(
        left, right, (((1,), (1,)), ((), ())), preferred_element_type=jnp.float32
    )


def rounded(value):
    return value.astype(jnp.bfloat16)


def merge_trans(upper_t, lower_t):
    return rounded(matmul(upper_t, lower_t))


def fetch(even_ref, odd_ref, target, sems, odd):
    rows = target.shape[0] // BLOCKS

    def start(ref):
        for j in range(BLOCKS):
            at = pl.ds(j * rows, rows)
            pltpu.make_async_copy(ref.at[at, :], target.at[at, :], sems.at[j]).start()

    pl.when(jnp.logical_not(odd))(lambda: start(even_ref))
    pl.when(odd)(lambda: start(odd_ref))


def arrived(ref, target, sems, j):
    rows = target.shape[0] // BLOCKS
    at = pl.ds(j * rows, rows)
    pltpu.make_async_copy(ref.at[at, :], target.at[at, :], sems.at[j]).wait()


def streamed(left, ref, target, sems):
    rows = target.shape[0] // BLOCKS
    total = None
    for j in range(BLOCKS):
        arrived(ref, target, sems, j)
        part = matmul(left[:, j * rows : (j + 1) * rows], target[pl.ds(j * rows, rows), :])
        total = part if total is None else total + part
    return total


def echo_kernel(down, trans, other_t, refl, other_r, out, upper_t, upper_r, lower_r, sems):
    odd = lax.rem(lax.axis_index("sec"), 2) == 1
    fetch(trans, other_t, upper_t, sems.at[0], odd)
    fetch(other_r, refl, lower_r, sems.at[1], odd)
    fetch(refl, other_r, upper_r, sems.at[2], odd)
    field = down[...]
    through = rounded(streamed(field, trans, upper_t, sems.at[0]))
    back = rounded(streamed(through, refl, lower_r, sems.at[1]))
    direct = streamed(field, refl, upper_r, sems.at[2])
    out[...] = direct + matmul_nt(back, upper_t[...])


def echo_of(down, trans, other_t, refl, other_r):
    size = trans.shape[0]
    matrix = pltpu.VMEM((size, size), jnp.bfloat16)
    hbm = pl.BlockSpec(memory_space=pltpu.HBM)
    vmem = pl.BlockSpec(memory_space=pltpu.VMEM)
    return pl.pallas_call(
        echo_kernel,
        out_shape=jax.ShapeDtypeStruct(down.shape, jnp.float32),
        in_specs=[vmem, hbm, hbm, hbm, hbm],
        out_specs=vmem,
        scratch_shapes=[matrix, matrix, matrix, pltpu.SemaphoreType.DMA((3, BLOCKS))],
        compiler_params=pltpu.CompilerParams(vmem_limit_bytes=52 * 2**20),
        cost_estimate=pl.CostEstimate(
            flops=8 * down.shape[0] * size * size, bytes_accessed=6 * size * size, transcendentals=0
        ),
    )(down, trans, other_t, refl, other_r)


def shards(layer_trans, layer_refl, source_modes):
    position = lax.axis_index("sec")
    section = position // 2
    parity = position % 2
    is_upper = parity == 0
    sections = lax.axis_size("sec") // 2
    trans = layer_trans[0]
    refl = layer_refl[0]
    half = source_modes.shape[0] // 2

    columns = jnp.arange(trans.shape[0], dtype=jnp.int32)
    units = rounded(source_modes[:, None] == columns[None, :])
    picked = rounded(matmul(units, trans))
    picked = swap_cores(picked)
    first = rounded(matmul(picked, trans))
    first = jnp.where(is_upper, swap_cores(first[:half]), first[half:])

    other_t = swap_cores(trans)
    other_r = swap_cores(refl)
    incoming = swap_sections(first, 0, 1)
    merged_t = lax.cond(
        is_upper,
        lambda: merge_trans(trans, other_t),
        lambda: merge_trans(other_t, trans),
    )
    mine = jnp.where(is_upper, units[:half], units[half:])
    mine = jnp.where(section == 1, incoming, mine)
    for step in range(1, sections - 1):
        incoming = swap_sections(rounded(matmul(incoming, merged_t)), step, step + 1)
        mine = jnp.where(section == step + 1, incoming, mine)

    echo = echo_of(mine, trans, other_t, refl, other_r)

    value = rounded(echo)
    upgoing = value
    for step in range(sections - 2, -1, -1):
        incoming = swap_sections(value, step + 1, step)
        value = rounded(echo + matmul_nt(incoming, merged_t))
        upgoing = jnp.where(section == step, value, upgoing)
    return upgoing[None]


def solution(mesh):
    return jax.shard_map(
        shards,
        mesh=mesh,
        in_specs=(P("sec", None, None), P("sec", None, None), P("freq")),
        out_specs=P(("freq", "sec"), None, None),
        check_vma=False,
    )
```

```python
import jax
import jax.numpy as jnp
from jax import lax
from jax.experimental import pallas as pl
from jax.experimental.pallas import tpu as pltpu
from jax.sharding import PartitionSpec as P

BLOCKS = 4
KEEP = 1
VMEM = 52 * 2**20


def swap_cores(array):
    return lax.ppermute(array, "sec", [(i, i ^ 1) for i in range(lax.axis_size("sec"))])


def swap_sections(value, one, two):
    pairs = []
    for device in range(lax.axis_size("sec")):
        section, core = divmod(device, 2)
        if section == one:
            target = 2 * two + core
        elif section == two:
            target = 2 * one + core
        else:
            target = device ^ 1
        pairs.append((device, target))
    return lax.ppermute(value, "sec", pairs)


def matmul(left, right):
    return jnp.dot(left, right, preferred_element_type=jnp.float32)


def matmul_nt(left, right):
    return lax.dot_general(
        left, right, (((1,), (1,)), ((), ())), preferred_element_type=jnp.float32
    )


def rounded(value):
    return value.astype(jnp.bfloat16)


def merge_trans(upper_t, lower_t):
    return rounded(matmul(upper_t, lower_t))


def fetch(even_ref, odd_ref, target, sems, odd):
    rows = target.shape[0] // BLOCKS

    def start(ref):
        for j in range(BLOCKS):
            at = pl.ds(j * rows, rows)
            pltpu.make_async_copy(ref.at[at, :], target.at[at, :], sems.at[j]).start()

    pl.when(jnp.logical_not(odd))(lambda: start(even_ref))
    pl.when(odd)(lambda: start(odd_ref))


def arrived(ref, target, sems, j):
    rows = target.shape[0] // BLOCKS
    at = pl.ds(j * rows, rows)
    pltpu.make_async_copy(ref.at[at, :], target.at[at, :], sems.at[j]).wait()


def streamed(left, ref, target, sems):
    rows = target.shape[0] // BLOCKS
    total = None
    for j in range(BLOCKS):
        arrived(ref, target, sems, j)
        part = matmul(left[:, j * rows : (j + 1) * rows], target[pl.ds(j * rows, rows), :])
        total = part if total is None else total + part
    return total


def echo_kernel(down, trans, other_t, refl, other_r, out, upper_t, upper_r, lower_r, sems):
    odd = lax.rem(lax.axis_index("sec"), 2) == 1
    fetch(trans, other_t, upper_t, sems.at[0], odd)
    fetch(other_r, refl, lower_r, sems.at[1], odd)
    fetch(refl, other_r, upper_r, sems.at[2], odd)
    field = down[...]
    through = rounded(streamed(field, trans, upper_t, sems.at[0]))
    back = rounded(streamed(through, refl, lower_r, sems.at[1]))
    direct = streamed(field, refl, upper_r, sems.at[2])
    out[...] = direct + matmul_nt(back, upper_t[...])


def echo_of(down, trans, other_t, refl, other_r):
    size = trans.shape[0]
    matrix = pltpu.VMEM((size, size), jnp.bfloat16)
    hbm = pl.BlockSpec(memory_space=pltpu.HBM)
    vmem = pl.BlockSpec(memory_space=pltpu.VMEM)
    return pl.pallas_call(
        echo_kernel,
        out_shape=jax.ShapeDtypeStruct(down.shape, jnp.float32),
        in_specs=[vmem, hbm, hbm, hbm, hbm],
        out_specs=vmem,
        scratch_shapes=[matrix, matrix, matrix, pltpu.SemaphoreType.DMA((3, BLOCKS))],
        compiler_params=pltpu.CompilerParams(vmem_limit_bytes=VMEM),
        cost_estimate=pl.CostEstimate(
            flops=8 * down.shape[0] * size, bytes_accessed=6 * size, transcendentals=0
        ),
    )(down, trans, other_t, refl, other_r)


def refl_kernel(trans, other_t, refl, other_r, out, upper_t, lower_r, upper_r, inner, result, sems, more):
    odd = lax.rem(lax.axis_index("sec"), 2) == 1
    rows, half = result.shape
    fetch(trans, other_t, upper_t, sems.at[0], odd)
    fetch(other_r, refl, lower_r, sems.at[1], odd)
    pl.when(jnp.logical_not(odd))(
        lambda: pltpu.make_async_copy(refl.at[:, pl.ds(0, half)], upper_r, more.at[0]).start()
    )
    pl.when(odd)(
        lambda: pltpu.make_async_copy(other_r.at[:, pl.ds(half, half)], upper_r, more.at[0]).start()
    )
    for j in range(BLOCKS):
        arrived(trans, upper_t, sems.at[0], j)
    start = pl.multiple_of(lax.rem(lax.axis_index("sec"), 2) * half, half)
    mine = upper_t[pl.ds(start, half), :]
    step = rows // BLOCKS
    for j in range(BLOCKS):
        arrived(refl, lower_r, sems.at[1], j)
        at = pl.ds(j * step, step)
        inner[at, :] = rounded(matmul_nt(lower_r[at, :], mine))
    pltpu.make_async_copy(refl.at[:, pl.ds(0, half)], upper_r, more.at[0]).wait()
    for j in range(BLOCKS):
        at = pl.ds(j * step, step)
        total = matmul(upper_t[at, :], inner[...])
        result[at, :] = rounded(upper_r[at, :].astype(jnp.float32) + total)
        pltpu.make_async_copy(result.at[at, :], out.at[at, :], more.at[1 + j]).start()
    for j in range(BLOCKS):
        at = pl.ds(j * step, step)
        pltpu.make_async_copy(result.at[at, :], out.at[at, :], more.at[1 + j]).wait()


def merge_refl(trans, other_t, refl, other_r):
    size = trans.shape[0]
    matrix = pltpu.VMEM((size, size), jnp.bfloat16)
    part = pltpu.VMEM((size, size // 2), jnp.bfloat16)
    hbm = pl.BlockSpec(memory_space=pltpu.HBM)
    return pl.pallas_call(
        refl_kernel,
        out_shape=jax.ShapeDtypeStruct((size, size // 2), jnp.bfloat16),
        in_specs=[hbm] * 4,
        out_specs=hbm,
        scratch_shapes=[
            matrix,
            matrix,
            part,
            part,
            part,
            pltpu.SemaphoreType.DMA((2, BLOCKS)),
            pltpu.SemaphoreType.DMA((1 + BLOCKS,)),
        ],
        compiler_params=pltpu.CompilerParams(vmem_limit_bytes=VMEM),
        cost_estimate=pl.CostEstimate(
            flops=2 * size**3, bytes_accessed=6 * size * size, transcendentals=0
        ),
    )(trans, other_t, refl, other_r)


def shards(layer_trans, layer_refl, source_modes):
    position = lax.axis_index("sec")
    section = position // 2
    parity = position % 2
    is_upper = parity == 0
    sections = lax.axis_size("sec") // 2
    trans = layer_trans[0]
    refl = layer_refl[0]
    half = source_modes.shape[0] // 2

    other_t = swap_cores(trans)
    other_r = swap_cores(refl)
    my_modes = lax.dynamic_slice_in_dim(source_modes, parity * half, half, 0)
    columns = jnp.arange(trans.shape[0], dtype=jnp.int32)
    incoming = rounded(my_modes[:, None] == columns[None, :])
    mine = incoming
    last = sections - 1
    merged_t = lax.switch(
        jnp.where(section == last, 2, parity),
        [
            lambda: merge_trans(trans, other_t),
            lambda: merge_trans(other_t, trans),
            lambda: trans,
        ],
    )
    other_r, merged_t = lax.optimization_barrier((other_r, merged_t))
    refl_half = lax.cond(
        section == last,
        lambda: merge_refl(trans, other_t, refl, other_r),
        lambda: jnp.zeros((trans.shape[0], trans.shape[1] // 2), jnp.bfloat16),
    )
    merged_t, refl_half = lax.optimization_barrier((merged_t, refl_half))

    def descend(first_step, stop, incoming):
        passed = []
        for step in range(first_step, stop):
            incoming = swap_sections(rounded(matmul(incoming, merged_t)), step, step + 1)
            passed.append(incoming)
        return passed

    next_half = swap_sections(refl_half, last - 1, last)
    fields = descend(0, KEEP, incoming)
    fields += lax.cond(
        source_modes[0] >= 0,
        lambda: descend(KEEP, last - 2, fields[-1]),
        lambda: [fields[-1]] * (last - 2 - KEEP),
    )
    after, *fields = lax.optimization_barrier((rounded(matmul(fields[-1], merged_t)), *fields))
    for step, field in enumerate(fields):
        mine = jnp.where(section == step + 1, field, mine)
    echo = echo_of(mine, trans, other_t, refl, other_r)
    incoming = swap_sections(after, last - 2, last - 1)
    incoming, echo = lax.optimization_barrier((incoming, echo))
    mine = jnp.where(section == last - 1, incoming, mine)
    echo = lax.cond(
        section == last - 1,
        lambda: echo_of(mine, trans, other_t, refl, other_r),
        lambda: echo,
    )
    below = rounded(matmul(mine, merged_t))
    below = jnp.concatenate([below, swap_cores(below)], 0)
    echo, next_half = lax.optimization_barrier((echo, next_half))
    part = rounded(matmul(below, next_half))
    kept, passed = part[:half], swap_cores(part[half:])
    up_last = jnp.concatenate(
        [jnp.where(is_upper, kept, passed), jnp.where(is_upper, passed, kept)], 1
    )
    value = rounded(echo + matmul_nt(up_last, merged_t))
    upgoing = jnp.where(section == last, swap_sections(up_last, last - 1, last), value)
    for step in range(last - 2, -1, -1):
        incoming = swap_sections(value, step + 1, step)
        value = rounded(echo + matmul_nt(incoming, merged_t))
        upgoing = jnp.where(section == step, value, upgoing)
    return upgoing[None]


def solution(mesh):
    return jax.shard_map(
        shards,
        mesh=mesh,
        in_specs=(P("sec", None, None), P("sec", None, None), P("freq")),
        out_specs=P(("freq", "sec"), None, None),
        check_vma=False,
    )
```

```python
import jax
import jax.numpy as jnp
from jax import lax
from jax.experimental import pallas as pl
from jax.experimental.pallas import tpu as pltpu
from jax.sharding import PartitionSpec as P

BLOCKS = 4
KEEP = 3
VMEM = 52 * 2**20


def swap_cores(array):
    return lax.ppermute(array, "sec", [(i, i ^ 1) for i in range(lax.axis_size("sec"))])


def swap_sections(value, one, two):
    pairs = []
    for device in range(lax.axis_size("sec")):
        section, core = divmod(device, 2)
        if section == one:
            target = 2 * two + core
        elif section == two:
            target = 2 * one + core
        else:
            target = device ^ 1
        pairs.append((device, target))
    return lax.ppermute(value, "sec", pairs)


def matmul(left, right):
    return jnp.dot(left, right, preferred_element_type=jnp.float32)


def matmul_nt(left, right):
    return lax.dot_general(
        left, right, (((1,), (1,)), ((), ())), preferred_element_type=jnp.float32
    )


def rounded(value):
    return value.astype(jnp.bfloat16)


def merge_trans(upper_t, lower_t):
    return rounded(matmul(upper_t, lower_t))


def fetch(even_ref, odd_ref, target, sems, odd):
    rows = target.shape[0] // BLOCKS

    def start(ref):
        for j in range(BLOCKS):
            at = pl.ds(j * rows, rows)
            pltpu.make_async_copy(ref.at[at, :], target.at[at, :], sems.at[j]).start()

    pl.when(jnp.logical_not(odd))(lambda: start(even_ref))
    pl.when(odd)(lambda: start(odd_ref))


def arrived(ref, target, sems, j):
    rows = target.shape[0] // BLOCKS
    at = pl.ds(j * rows, rows)
    pltpu.make_async_copy(ref.at[at, :], target.at[at, :], sems.at[j]).wait()


def streamed(left, ref, target, sems):
    rows = target.shape[0] // BLOCKS
    total = None
    for j in range(BLOCKS):
        arrived(ref, target, sems, j)
        part = matmul(left[:, j * rows : (j + 1) * rows], target[pl.ds(j * rows, rows), :])
        total = part if total is None else total + part
    return total


def echo_kernel(down, trans, other_t, refl, other_r, out, upper_t, upper_r, lower_r, sems):
    odd = lax.rem(lax.axis_index("sec"), 2) == 1
    fetch(trans, other_t, upper_t, sems.at[0], odd)
    fetch(other_r, refl, lower_r, sems.at[1], odd)
    fetch(refl, other_r, upper_r, sems.at[2], odd)
    field = down[...]
    through = rounded(streamed(field, trans, upper_t, sems.at[0]))
    back = rounded(streamed(through, refl, lower_r, sems.at[1]))
    direct = streamed(field, refl, upper_r, sems.at[2])
    out[...] = direct + matmul_nt(back, upper_t[...])


def echo_of(down, trans, other_t, refl, other_r):
    size = trans.shape[0]
    matrix = pltpu.VMEM((size, size), jnp.bfloat16)
    hbm = pl.BlockSpec(memory_space=pltpu.HBM)
    vmem = pl.BlockSpec(memory_space=pltpu.VMEM)
    return pl.pallas_call(
        echo_kernel,
        out_shape=jax.ShapeDtypeStruct(down.shape, jnp.float32),
        in_specs=[vmem, hbm, hbm, hbm, hbm],
        out_specs=vmem,
        scratch_shapes=[matrix, matrix, matrix, pltpu.SemaphoreType.DMA((3, BLOCKS))],
        compiler_params=pltpu.CompilerParams(vmem_limit_bytes=VMEM),
        cost_estimate=pl.CostEstimate(
            flops=8 * down.shape[0] * size, bytes_accessed=6 * size, transcendentals=0
        ),
    )(down, trans, other_t, refl, other_r)


def refl_kernel(trans, other_t, refl, other_r, out, upper_t, lower_r, upper_r, inner, result, sems, more):
    odd = lax.rem(lax.axis_index("sec"), 2) == 1
    rows, half = result.shape
    fetch(trans, other_t, upper_t, sems.at[0], odd)
    fetch(other_r, refl, lower_r, sems.at[1], odd)
    pl.when(jnp.logical_not(odd))(
        lambda: pltpu.make_async_copy(refl.at[:, pl.ds(0, half)], upper_r, more.at[0]).start()
    )
    pl.when(odd)(
        lambda: pltpu.make_async_copy(other_r.at[:, pl.ds(half, half)], upper_r, more.at[0]).start()
    )
    for j in range(BLOCKS):
        arrived(trans, upper_t, sems.at[0], j)
    start = pl.multiple_of(lax.rem(lax.axis_index("sec"), 2) * half, half)
    mine = upper_t[pl.ds(start, half), :]
    step = rows // BLOCKS
    for j in range(BLOCKS):
        arrived(refl, lower_r, sems.at[1], j)
        at = pl.ds(j * step, step)
        inner[at, :] = rounded(matmul_nt(lower_r[at, :], mine))
    pltpu.make_async_copy(refl.at[:, pl.ds(0, half)], upper_r, more.at[0]).wait()
    for j in range(BLOCKS):
        at = pl.ds(j * step, step)
        total = matmul(upper_t[at, :], inner[...])
        result[at, :] = rounded(upper_r[at, :].astype(jnp.float32) + total)
        pltpu.make_async_copy(result.at[at, :], out.at[at, :], more.at[1 + j]).start()
    for j in range(BLOCKS):
        at = pl.ds(j * step, step)
        pltpu.make_async_copy(result.at[at, :], out.at[at, :], more.at[1 + j]).wait()


def merge_refl(trans, other_t, refl, other_r):
    size = trans.shape[0]
    matrix = pltpu.VMEM((size, size), jnp.bfloat16)
    part = pltpu.VMEM((size, size // 2), jnp.bfloat16)
    hbm = pl.BlockSpec(memory_space=pltpu.HBM)
    return pl.pallas_call(
        refl_kernel,
        out_shape=jax.ShapeDtypeStruct((size, size // 2), jnp.bfloat16),
        in_specs=[hbm] * 4,
        out_specs=hbm,
        scratch_shapes=[
            matrix,
            matrix,
            part,
            part,
            part,
            pltpu.SemaphoreType.DMA((2, BLOCKS)),
            pltpu.SemaphoreType.DMA((1 + BLOCKS,)),
        ],
        compiler_params=pltpu.CompilerParams(vmem_limit_bytes=VMEM),
        cost_estimate=pl.CostEstimate(
            flops=2 * size**3, bytes_accessed=6 * size * size, transcendentals=0
        ),
    )(trans, other_t, refl, other_r)


def shards(layer_trans, layer_refl, source_modes):
    position = lax.axis_index("sec")
    section = position // 2
    parity = position % 2
    is_upper = parity == 0
    sections = lax.axis_size("sec") // 2
    trans = layer_trans[0]
    refl = layer_refl[0]
    half = source_modes.shape[0] // 2

    other_t = swap_cores(trans)
    other_r = swap_cores(refl)
    my_modes = lax.dynamic_slice_in_dim(source_modes, parity * half, half, 0)
    columns = jnp.arange(trans.shape[0], dtype=jnp.int32)
    incoming = rounded(my_modes[:, None] == columns[None, :])
    mine = incoming
    last = sections - 1
    merged_t = lax.switch(
        jnp.where(section == last, 2, parity),
        [
            lambda: merge_trans(trans, other_t),
            lambda: merge_trans(other_t, trans),
            lambda: trans,
        ],
    )
    other_r, merged_t = lax.optimization_barrier((other_r, merged_t))
    refl_half = lax.cond(
        section == last,
        lambda: merge_refl(trans, other_t, refl, other_r),
        lambda: jnp.zeros((trans.shape[0], trans.shape[1] // 2), jnp.bfloat16),
    )
    merged_t, refl_half = lax.optimization_barrier((merged_t, refl_half))

    def descend(first_step, stop, incoming):
        passed = []
        for step in range(first_step, stop):
            incoming = swap_sections(rounded(matmul(incoming, merged_t)), step, step + 1)
            passed.append(incoming)
        return passed

    next_half = swap_sections(refl_half, last - 1, last)
    fields = descend(0, KEEP, incoming)
    fields += lax.cond(
        source_modes[0] >= 0,
        lambda: descend(KEEP, last - 2, fields[-1]),
        lambda: [fields[-1]] * (last - 2 - KEEP),
    )
    after, *fields = lax.optimization_barrier((rounded(matmul(fields[-1], merged_t)), *fields))
    for step, field in enumerate(fields):
        mine = jnp.where(section == step + 1, field, mine)
    echo = echo_of(mine, trans, other_t, refl, other_r)
    incoming = swap_sections(after, last - 2, last - 1)
    incoming, echo = lax.optimization_barrier((incoming, echo))
    mine = jnp.where(section == last - 1, incoming, mine)
    echo = lax.cond(
        section == last - 1,
        lambda: echo_of(mine, trans, other_t, refl, other_r),
        lambda: echo,
    )
    below = rounded(matmul(mine, merged_t))
    below = jnp.concatenate([below, swap_cores(below)], 0)
    echo, next_half = lax.optimization_barrier((echo, next_half))
    part = rounded(matmul(below, next_half))
    kept, passed = part[:half], swap_cores(part[half:])
    up_last = jnp.concatenate(
        [jnp.where(is_upper, kept, passed), jnp.where(is_upper, passed, kept)], 1
    )
    value = rounded(echo + matmul_nt(up_last, merged_t))
    upgoing = jnp.where(section == last, swap_sections(up_last, last - 1, last), value)
    for step in range(last - 2, -1, -1):
        incoming = swap_sections(value, step + 1, step)
        value = rounded(echo + matmul_nt(incoming, merged_t))
        upgoing = jnp.where(section == step, value, upgoing)
    return upgoing[None]


def solution(mesh):
    return jax.shard_map(
        shards,
        mesh=mesh,
        in_specs=(P("sec", None, None), P("sec", None, None), P("freq")),
        out_specs=P(("freq", "sec"), None, None),
        check_vma=False,
    )
```

```python
import jax
import jax.numpy as jnp
from jax import lax
from jax.experimental import pallas as pl
from jax.experimental.pallas import tpu as pltpu
from jax.sharding import PartitionSpec as P

BLOCKS = 4
KEEP = 3
VMEM = 52 * 2**20


def swap_cores(array):
    return lax.ppermute(array, "sec", [(i, i ^ 1) for i in range(lax.axis_size("sec"))])


def swap_sections(value, one, two):
    pairs = []
    for device in range(lax.axis_size("sec")):
        section, core = divmod(device, 2)
        if section == one:
            target = 2 * two + core
        elif section == two:
            target = 2 * one + core
        else:
            target = device ^ 1
        pairs.append((device, target))
    return lax.ppermute(value, "sec", pairs)


def matmul(left, right):
    return jnp.dot(left, right, preferred_element_type=jnp.float32)


def matmul_nt(left, right):
    return lax.dot_general(
        left, right, (((1,), (1,)), ((), ())), preferred_element_type=jnp.float32
    )


def rounded(value):
    return value.astype(jnp.bfloat16)


def merge_trans(upper_t, lower_t):
    return rounded(matmul(upper_t, lower_t))


def fetch(even_ref, odd_ref, target, sems, odd):
    rows = target.shape[0] // BLOCKS

    def start(ref):
        for j in range(BLOCKS):
            at = pl.ds(j * rows, rows)
            pltpu.make_async_copy(ref.at[at, :], target.at[at, :], sems.at[j]).start()

    pl.when(jnp.logical_not(odd))(lambda: start(even_ref))
    pl.when(odd)(lambda: start(odd_ref))


def arrived(ref, target, sems, j):
    rows = target.shape[0] // BLOCKS
    at = pl.ds(j * rows, rows)
    pltpu.make_async_copy(ref.at[at, :], target.at[at, :], sems.at[j]).wait()


def streamed(left, ref, target, sems):
    rows = target.shape[0] // BLOCKS
    total = None
    for j in range(BLOCKS):
        arrived(ref, target, sems, j)
        part = matmul(left[:, j * rows : (j + 1) * rows], target[pl.ds(j * rows, rows), :])
        total = part if total is None else total + part
    return total


def echo_kernel(down, trans, other_t, refl, other_r, out, upper_t, upper_r, lower_r, sems):
    odd = lax.rem(lax.axis_index("sec"), 2) == 1
    fetch(trans, other_t, upper_t, sems.at[0], odd)
    fetch(other_r, refl, lower_r, sems.at[1], odd)
    fetch(refl, other_r, upper_r, sems.at[2], odd)
    field = down[...]
    through = rounded(streamed(field, trans, upper_t, sems.at[0]))
    back = rounded(streamed(through, refl, lower_r, sems.at[1]))
    direct = streamed(field, refl, upper_r, sems.at[2])
    out[...] = direct + matmul_nt(back, upper_t[...])


def echo_of(down, trans, other_t, refl, other_r):
    size = trans.shape[0]
    matrix = pltpu.VMEM((size, size), jnp.bfloat16)
    hbm = pl.BlockSpec(memory_space=pltpu.HBM)
    vmem = pl.BlockSpec(memory_space=pltpu.VMEM)
    return pl.pallas_call(
        echo_kernel,
        out_shape=jax.ShapeDtypeStruct(down.shape, jnp.float32),
        in_specs=[vmem, hbm, hbm, hbm, hbm],
        out_specs=vmem,
        scratch_shapes=[matrix, matrix, matrix, pltpu.SemaphoreType.DMA((3, BLOCKS))],
        compiler_params=pltpu.CompilerParams(vmem_limit_bytes=VMEM),
        cost_estimate=pl.CostEstimate(
            flops=8 * down.shape[0] * size, bytes_accessed=6 * size, transcendentals=0
        ),
    )(down, trans, other_t, refl, other_r)


def refl_kernel(trans, other_t, refl, other_r, out, upper_t, lower_r, upper_r, inner, result, sems, more):
    odd = lax.rem(lax.axis_index("sec"), 2) == 1
    rows, half = result.shape
    fetch(trans, other_t, upper_t, sems.at[0], odd)
    fetch(other_r, refl, lower_r, sems.at[1], odd)
    pl.when(jnp.logical_not(odd))(
        lambda: pltpu.make_async_copy(refl.at[:, pl.ds(0, half)], upper_r, more.at[0]).start()
    )
    pl.when(odd)(
        lambda: pltpu.make_async_copy(other_r.at[:, pl.ds(half, half)], upper_r, more.at[0]).start()
    )
    for j in range(BLOCKS):
        arrived(trans, upper_t, sems.at[0], j)
    start = pl.multiple_of(lax.rem(lax.axis_index("sec"), 2) * half, half)
    mine = upper_t[pl.ds(start, half), :]
    step = rows // BLOCKS
    for j in range(BLOCKS):
        arrived(refl, lower_r, sems.at[1], j)
        at = pl.ds(j * step, step)
        inner[at, :] = rounded(matmul_nt(lower_r[at, :], mine))
    pltpu.make_async_copy(refl.at[:, pl.ds(0, half)], upper_r, more.at[0]).wait()
    for j in range(BLOCKS):
        at = pl.ds(j * step, step)
        total = matmul(upper_t[at, :], inner[...])
        result[at, :] = rounded(upper_r[at, :].astype(jnp.float32) + total)
        pltpu.make_async_copy(result.at[at, :], out.at[at, :], more.at[1 + j]).start()
    for j in range(BLOCKS):
        at = pl.ds(j * step, step)
        pltpu.make_async_copy(result.at[at, :], out.at[at, :], more.at[1 + j]).wait()


def merge_refl(trans, other_t, refl, other_r):
    size = trans.shape[0]
    matrix = pltpu.VMEM((size, size), jnp.bfloat16)
    part = pltpu.VMEM((size, size // 2), jnp.bfloat16)
    hbm = pl.BlockSpec(memory_space=pltpu.HBM)
    return pl.pallas_call(
        refl_kernel,
        out_shape=jax.ShapeDtypeStruct((size, size // 2), jnp.bfloat16),
        in_specs=[hbm] * 4,
        out_specs=hbm,
        scratch_shapes=[
            matrix,
            matrix,
            part,
            part,
            part,
            pltpu.SemaphoreType.DMA((2, BLOCKS)),
            pltpu.SemaphoreType.DMA((1 + BLOCKS,)),
        ],
        compiler_params=pltpu.CompilerParams(vmem_limit_bytes=VMEM),
        cost_estimate=pl.CostEstimate(
            flops=2 * size**3, bytes_accessed=6 * size * size, transcendentals=0
        ),
    )(trans, other_t, refl, other_r)


def shards(layer_trans, layer_refl, source_modes):
    position = lax.axis_index("sec")
    section = position // 2
    parity = position % 2
    is_upper = parity == 0
    sections = lax.axis_size("sec") // 2
    trans = layer_trans[0]
    refl = layer_refl[0]
    half = source_modes.shape[0] // 2

    other_t = swap_cores(trans)
    other_r = swap_cores(refl)
    my_modes = lax.dynamic_slice_in_dim(source_modes, parity * half, half, 0)
    columns = jnp.arange(trans.shape[0], dtype=jnp.int32)
    incoming = rounded(my_modes[:, None] == columns[None, :])
    mine = incoming
    last = sections - 1
    merged_t = lax.switch(
        jnp.where(section == last, 2, parity),
        [
            lambda: merge_trans(trans, other_t),
            lambda: merge_trans(other_t, trans),
            lambda: trans,
        ],
    )
    other_r, merged_t = lax.optimization_barrier((other_r, merged_t))
    refl_half = lax.cond(
        section == last,
        lambda: merge_refl(trans, other_t, refl, other_r),
        lambda: jnp.zeros((trans.shape[0], trans.shape[1] // 2), jnp.bfloat16),
    )
    merged_t, refl_half = lax.optimization_barrier((merged_t, refl_half))

    def descend(first_step, stop, incoming):
        passed = []
        for step in range(first_step, stop):
            incoming = swap_sections(rounded(matmul(incoming, merged_t)), step, step + 1)
            passed.append(incoming)
        return passed

    next_half = swap_sections(refl_half, last - 1, last)
    fields = descend(0, KEEP, incoming)
    fields += lax.cond(
        source_modes[0] >= 0,
        lambda: descend(KEEP, last - 2, fields[-1]),
        lambda: [fields[-1]] * (last - 2 - KEEP),
    )
    after, *fields = lax.optimization_barrier((rounded(matmul(fields[-1], merged_t)), *fields))
    for step, field in enumerate(fields):
        mine = jnp.where(section == step + 1, field, mine)
    echo = lax.cond(
        section == last - 1,
        lambda: jnp.zeros(mine.shape, jnp.float32),
        lambda: echo_of(mine, trans, other_t, refl, other_r),
    )
    incoming = swap_sections(after, last - 2, last - 1)
    incoming, echo = lax.optimization_barrier((incoming, echo))
    mine = jnp.where(section == last - 1, incoming, mine)
    echo = lax.cond(
        section == last - 1,
        lambda: echo_of(mine, trans, other_t, refl, other_r),
        lambda: echo,
    )
    below = rounded(matmul(mine, merged_t))
    below = jnp.concatenate([below, swap_cores(below)], 0)
    echo, next_half = lax.optimization_barrier((echo, next_half))
    part = rounded(matmul(below, next_half))
    kept, passed = part[:half], swap_cores(part[half:])
    up_last = jnp.concatenate(
        [jnp.where(is_upper, kept, passed), jnp.where(is_upper, passed, kept)], 1
    )
    value = rounded(echo + matmul_nt(up_last, merged_t))
    upgoing = jnp.where(section == last, swap_sections(up_last, last - 1, last), value)
    for step in range(last - 2, -1, -1):
        incoming = swap_sections(value, step + 1, step)
        value = rounded(echo + matmul_nt(incoming, merged_t))
        upgoing = jnp.where(section == step, value, upgoing)
    return upgoing[None]


def solution(mesh):
    return jax.shard_map(
        shards,
        mesh=mesh,
        in_specs=(P("sec", None, None), P("sec", None, None), P("freq")),
        out_specs=P(("freq", "sec"), None, None),
        check_vma=False,
    )
```

```python
import jax
import jax.numpy as jnp
from jax import lax
from jax.experimental import pallas as pl
from jax.experimental.pallas import tpu as pltpu
from jax.sharding import PartitionSpec as P

BLOCKS = 4
KEEP = 3
VMEM = 46 * 2**20


def swap_cores(array):
    return lax.ppermute(array, "sec", [(i, i ^ 1) for i in range(lax.axis_size("sec"))])


def swap_sections(value, one, two):
    pairs = []
    for device in range(lax.axis_size("sec")):
        section, core = divmod(device, 2)
        if section == one:
            target = 2 * two + core
        elif section == two:
            target = 2 * one + core
        else:
            target = device ^ 1
        pairs.append((device, target))
    return lax.ppermute(value, "sec", pairs)


def matmul(left, right):
    return jnp.dot(left, right, preferred_element_type=jnp.float32)


def matmul_nt(left, right):
    return lax.dot_general(
        left, right, (((1,), (1,)), ((), ())), preferred_element_type=jnp.float32
    )


def rounded(value):
    return value.astype(jnp.bfloat16)


def merge_trans(upper_t, lower_t):
    return rounded(matmul(upper_t, lower_t))


def fetch(even_ref, odd_ref, target, sems, odd):
    rows = target.shape[0] // BLOCKS

    def start(ref):
        for j in range(BLOCKS):
            at = pl.ds(j * rows, rows)
            pltpu.make_async_copy(ref.at[at, :], target.at[at, :], sems.at[j]).start()

    pl.when(jnp.logical_not(odd))(lambda: start(even_ref))
    pl.when(odd)(lambda: start(odd_ref))


def arrived(ref, target, sems, j):
    rows = target.shape[0] // BLOCKS
    at = pl.ds(j * rows, rows)
    pltpu.make_async_copy(ref.at[at, :], target.at[at, :], sems.at[j]).wait()


def streamed(left, ref, target, sems):
    rows = target.shape[0] // BLOCKS
    total = None
    for j in range(BLOCKS):
        arrived(ref, target, sems, j)
        part = matmul(left[:, j * rows : (j + 1) * rows], target[pl.ds(j * rows, rows), :])
        total = part if total is None else total + part
    return total


def echo_kernel(down, trans, other_t, refl, other_r, out, upper_t, upper_r, lower_r, sems):
    odd = lax.rem(lax.axis_index("sec"), 2) == 1
    fetch(trans, other_t, upper_t, sems.at[0], odd)
    fetch(other_r, refl, lower_r, sems.at[1], odd)
    fetch(refl, other_r, upper_r, sems.at[2], odd)
    field = down[...]
    through = rounded(streamed(field, trans, upper_t, sems.at[0]))
    back = rounded(streamed(through, refl, lower_r, sems.at[1]))
    direct = streamed(field, refl, upper_r, sems.at[2])
    out[...] = direct + matmul_nt(back, upper_t[...])


def echo_of(down, trans, other_t, refl, other_r):
    size = trans.shape[0]
    matrix = pltpu.VMEM((size, size), jnp.bfloat16)
    hbm = pl.BlockSpec(memory_space=pltpu.HBM)
    vmem = pl.BlockSpec(memory_space=pltpu.VMEM)
    return pl.pallas_call(
        echo_kernel,
        out_shape=jax.ShapeDtypeStruct(down.shape, jnp.float32),
        in_specs=[vmem, hbm, hbm, hbm, hbm],
        out_specs=vmem,
        scratch_shapes=[matrix, matrix, matrix, pltpu.SemaphoreType.DMA((3, BLOCKS))],
        compiler_params=pltpu.CompilerParams(vmem_limit_bytes=VMEM),
        cost_estimate=pl.CostEstimate(
            flops=8 * down.shape[0] * size, bytes_accessed=6 * size, transcendentals=0
        ),
    )(down, trans, other_t, refl, other_r)


def refl_kernel(trans, other_t, refl, other_r, out, upper_t, lower_r, upper_r, inner, result, sems, more):
    odd = lax.rem(lax.axis_index("sec"), 2) == 1
    rows, half = result.shape
    fetch(trans, other_t, upper_t, sems.at[0], odd)
    fetch(other_r, refl, lower_r, sems.at[1], odd)
    pl.when(jnp.logical_not(odd))(
        lambda: pltpu.make_async_copy(refl.at[:, pl.ds(0, half)], upper_r, more.at[0]).start()
    )
    pl.when(odd)(
        lambda: pltpu.make_async_copy(other_r.at[:, pl.ds(half, half)], upper_r, more.at[0]).start()
    )
    for j in range(BLOCKS):
        arrived(trans, upper_t, sems.at[0], j)
    start = pl.multiple_of(lax.rem(lax.axis_index("sec"), 2) * half, half)
    mine = upper_t[pl.ds(start, half), :]
    step = rows // BLOCKS
    for j in range(BLOCKS):
        arrived(refl, lower_r, sems.at[1], j)
        at = pl.ds(j * step, step)
        inner[at, :] = rounded(matmul_nt(lower_r[at, :], mine))
    pltpu.make_async_copy(refl.at[:, pl.ds(0, half)], upper_r, more.at[0]).wait()
    for j in range(BLOCKS):
        at = pl.ds(j * step, step)
        total = matmul(upper_t[at, :], inner[...])
        result[at, :] = rounded(upper_r[at, :].astype(jnp.float32) + total)
        pltpu.make_async_copy(result.at[at, :], out.at[at, :], more.at[1 + j]).start()
    for j in range(BLOCKS):
        at = pl.ds(j * step, step)
        pltpu.make_async_copy(result.at[at, :], out.at[at, :], more.at[1 + j]).wait()


def merge_refl(trans, other_t, refl, other_r):
    size = trans.shape[0]
    matrix = pltpu.VMEM((size, size), jnp.bfloat16)
    part = pltpu.VMEM((size, size // 2), jnp.bfloat16)
    hbm = pl.BlockSpec(memory_space=pltpu.HBM)
    return pl.pallas_call(
        refl_kernel,
        out_shape=jax.ShapeDtypeStruct((size, size // 2), jnp.bfloat16),
        in_specs=[hbm] * 4,
        out_specs=hbm,
        scratch_shapes=[
            matrix,
            matrix,
            part,
            part,
            part,
            pltpu.SemaphoreType.DMA((2, BLOCKS)),
            pltpu.SemaphoreType.DMA((1 + BLOCKS,)),
        ],
        compiler_params=pltpu.CompilerParams(vmem_limit_bytes=VMEM),
        cost_estimate=pl.CostEstimate(
            flops=2 * size**3, bytes_accessed=6 * size * size, transcendentals=0
        ),
    )(trans, other_t, refl, other_r)


def shards(layer_trans, layer_refl, source_modes):
    position = lax.axis_index("sec")
    section = position // 2
    parity = position % 2
    is_upper = parity == 0
    sections = lax.axis_size("sec") // 2
    trans = layer_trans[0]
    refl = layer_refl[0]
    half = source_modes.shape[0] // 2

    other_t = swap_cores(trans)
    other_r = swap_cores(refl)
    my_modes = lax.dynamic_slice_in_dim(source_modes, parity * half, half, 0)
    columns = jnp.arange(trans.shape[0], dtype=jnp.int32)
    incoming = rounded(my_modes[:, None] == columns[None, :])
    mine = incoming
    last = sections - 1
    merged_t = lax.switch(
        jnp.where(section == last, 2, parity),
        [
            lambda: merge_trans(trans, other_t),
            lambda: merge_trans(other_t, trans),
            lambda: trans,
        ],
    )
    other_r, merged_t = lax.optimization_barrier((other_r, merged_t))
    refl_half = lax.cond(
        section == last,
        lambda: merge_refl(trans, other_t, refl, other_r),
        lambda: jnp.zeros((trans.shape[0], trans.shape[1] // 2), jnp.bfloat16),
    )
    merged_t, refl_half = lax.optimization_barrier((merged_t, refl_half))

    def descend(first_step, stop, incoming):
        passed = []
        for step in range(first_step, stop):
            incoming = swap_sections(rounded(matmul(incoming, merged_t)), step, step + 1)
            passed.append(incoming)
        return passed

    next_half = swap_sections(refl_half, last - 1, last)
    fields = descend(0, KEEP, incoming)
    fields += lax.cond(
        source_modes[0] >= 0,
        lambda: descend(KEEP, last - 2, fields[-1]),
        lambda: [fields[-1]] * (last - 2 - KEEP),
    )
    after, *fields = lax.optimization_barrier((rounded(matmul(fields[-1], merged_t)), *fields))
    for step, field in enumerate(fields):
        mine = jnp.where(section == step + 1, field, mine)
    echo = echo_of(mine, trans, other_t, refl, other_r)
    incoming = swap_sections(after, last - 2, last - 1)
    incoming, echo = lax.optimization_barrier((incoming, echo))
    mine = jnp.where(section == last - 1, incoming, mine)
    echo = lax.cond(
        section == last - 1,
        lambda: echo_of(mine, trans, other_t, refl, other_r),
        lambda: echo,
    )
    below = rounded(matmul(mine, merged_t))
    below = jnp.concatenate([below, swap_cores(below)], 0)
    echo, next_half = lax.optimization_barrier((echo, next_half))
    part = rounded(matmul(below, next_half))
    kept, passed = part[:half], swap_cores(part[half:])
    up_last = jnp.concatenate(
        [jnp.where(is_upper, kept, passed), jnp.where(is_upper, passed, kept)], 1
    )
    value = rounded(echo + matmul_nt(up_last, merged_t))
    upgoing = jnp.where(section == last, swap_sections(up_last, last - 1, last), value)
    for step in range(last - 2, -1, -1):
        incoming = swap_sections(value, step + 1, step)
        value = rounded(echo + matmul_nt(incoming, merged_t))
        upgoing = jnp.where(section == step, value, upgoing)
    return upgoing[None]


def solution(mesh):
    return jax.shard_map(
        shards,
        mesh=mesh,
        in_specs=(P("sec", None, None), P("sec", None, None), P("freq")),
        out_specs=P(("freq", "sec"), None, None),
        check_vma=False,
    )
```
